32 devices in a mesh: mem: 8 (over z, y), lat: 4 (over x, core).
Axes of the slice: x: 2, y: 2, z: 4, core: 2. Of those that a mesh axis runs over, the one named last changes fastest.
Arguments:
- prior_sample_states: bfloat16 [16, 2, 16, 1024], P('mem', None, 'lat'), may hold values from -6 to 6
- wind_cfl_ratios: float32 [2, 16, 1024], P(None, 'lat'), may hold values from -0.45 to 0.45
- obs_cell: int32 [4, 2048], P('lat', 'mem'), may hold values from 0 to 511
- obs_value: float32 [4, 2048], P('lat', 'mem'), may hold values from -6 to 6
- obs_precision: float32 [4, 2048], P('lat', 'mem'), may hold values from 0.25 to 4
- neighbours: int32 [16, 8, 512], P('lat', 'mem'), may hold values from 0 to 1279, as said below
- obs_counts: int32 [16, 8], P('lat', 'mem'), may hold values from 128 to 512, as said below
Outputs:
- analysis: bfloat16 [16, 2, 16, 1024], P('mem', None, 'lat')
The draws below stay inside these ranges and needn't reach their ends.
Inputs may be any that keep to these rules, and one draw needn't show every extreme that they name: `obs_counts`: in every tile some block's list has all 512 slots live. `neighbours`: the 512 entries of one list are distinct and index the extended set of its tile.
All inputs are finite; a program needn't handle non-finite values. Where the reference program divides by a largest or mean magnitude, that divisor is 1e-20 or more.
Results may differ from the reference program's by a relative error of at most 0.0053.
Values may be sent and summed in bfloat16 or wider, within the bound.
A program may use at most 64 MiB of HBM per device.

```python
import math
import jax
import jax.numpy as jnp
from jax import lax

ENS = 16
ZONE_HEIGHT = 4
PATCH_WIDTH = 128
OBS_DEV = 256
KNB = 512
SECTIONS = 4
NS_ITERS = 6
MESH_HEIGHT = 16
MESH_WIDTH = 1024
LOC_ROWS = 2
LOC_COLS = 64
N_MEM = 8
N_LAT = 4


def draw_neighbours(key, part):
    extent = 5 * OBS_DEV
    tile_total = MESH_WIDTH // PATCH_WIDTH
    scores = jax.random.randint(key, (MESH_HEIGHT, tile_total, extent), 0, 1024)
    scores = scores * extent + jnp.arange(extent, dtype=jnp.int32)
    top_values, top_index = lax.top_k(scores, KNB)
    return top_index.astype(jnp.int32)


def draw_obs_counts(key, part):
    band_total = MESH_HEIGHT // ZONE_HEIGHT
    tile_total = MESH_WIDTH // PATCH_WIDTH
    counts = jax.random.randint(key, (band_total, ZONE_HEIGHT, tile_total), KNB // 4, KNB + 1)
    picked = jax.random.randint(jax.random.fold_in(key, 7), (band_total, 1, tile_total), 0, ZONE_HEIGHT)
    counts = jnp.where(jnp.arange(ZONE_HEIGHT, dtype=jnp.int32)[None, :, None] == picked, KNB, counts)
    return counts.reshape(MESH_HEIGHT, tile_total).astype(jnp.int32)


def plant(values, key, low, top_value):
    place = [jax.random.randint(jax.random.fold_in(key, axis), (), 0, length) for axis, length in enumerate(values.shape)]
    widest = values.shape.index(max(values.shape))
    beside = place[:widest] + [(place[widest] + 1) % values.shape[widest]] + place[widest + 1:]
    return values.at[tuple(place)].set(low).at[tuple(beside)].set(top_value)


def levels(rng, shape, split, least, high):
    gain, own = 1.0, jax.random.fold_in(rng, 6)
    for position, blocks in split:
        heights = jnp.exp(jax.random.uniform(jax.random.fold_in(own, position), (blocks,), jnp.float32, least / len(split), high / len(split)))
        gain = gain * jnp.repeat(heights, shape[position] // blocks).reshape([-1 if axis == position else 1 for axis in range(len(shape))])
    return gain


def scatter_about(own_key, dims, width, reach, cuts=(), kind=jnp.bfloat16):
    result = jax.random.normal(own_key, dims, jnp.float32) * width
    if len(cuts) > 0:
        result = levels(own_key, dims, cuts, -0.22, 0.18) * result
    return jnp.clip(result, min=-reach, max=reach).astype(kind)


def setup_inputs(seed: int = 0) -> dict:
    arg_keys = jax.random.split(jax.random.key(seed), 8)
    return {
        "prior_sample_states": scatter_about(arg_keys[0], (ENS, 2, MESH_HEIGHT, MESH_WIDTH), 1.0, 6.0, ((0, 8), (2, 4))),
        "wind_cfl_ratios": jnp.clip(jax.random.uniform(arg_keys[1], (2, MESH_HEIGHT, MESH_WIDTH), jnp.float32, -0.45, 0.45) * levels(arg_keys[1], (2, MESH_HEIGHT, MESH_WIDTH), ((1, 4),), -0.4, 0.0), -0.45, 0.45),
        "obs_cell": plant(jax.random.randint(arg_keys[2], (N_LAT, N_MEM * OBS_DEV), 0, ZONE_HEIGHT * PATCH_WIDTH), jax.random.fold_in(arg_keys[2], 1), 0, (ZONE_HEIGHT * PATCH_WIDTH) - 1).astype(jnp.int32),
        "obs_value": scatter_about(arg_keys[3], (N_LAT, N_MEM * OBS_DEV), 1.0, 6.0, ((0, 4), (1, 8)), jnp.float32),
        "obs_precision": jnp.clip(jnp.exp(math.log(4.0) - 2.7725887 * jax.random.uniform(arg_keys[4], (N_LAT, N_MEM * OBS_DEV), jnp.float32) ** levels(arg_keys[4], (N_LAT, N_MEM * OBS_DEV), ((0, 4), (1, 8)), -0.2, 0.2)), 0.25, 4.0),
        "neighbours": draw_neighbours(jax.random.fold_in(arg_keys[7], 71), 0),
        "obs_counts": draw_obs_counts(jax.random.fold_in(arg_keys[7], 71), 0),
    }


KAPPA = (0.025, 0.0125)
HIGHEST = lax.Precision.HIGHEST

def index_tuple(*entries):
    return tuple((jnp.asarray(entry).astype(jnp.int32) for entry in entries))

def advance(padded, east_wind, north_wind, diffusion):
    centre = padded[:, 1:-1, :]
    north_row = padded[:, 2:, :]
    south_row = padded[:, :-2, :]
    widened = jnp.pad(centre, ((0, 0), (0, 0), (1, 1)))
    west_cell = widened[:, :, :-2]
    east_cell = widened[:, :, 2:]
    transport = jnp.maximum(east_wind, 0.0) * (centre - west_cell) + jnp.minimum(east_wind, 0.0) * (east_cell - centre) + jnp.maximum(north_wind, 0.0) * (centre - south_row) + jnp.minimum(north_wind, 0.0) * (north_row - centre)
    return centre - transport + diffusion * (north_row + south_row + east_cell + west_cell - 4.0 * centre)

def place_piece(piece, sample_realizations, row_shift, col_shift):
    return jnp.concatenate([piece[:sample_realizations + 2], piece[sample_realizations + 2:sample_realizations + 3] + row_shift, piece[sample_realizations + 3:] + col_shift], axis=0)

def analyze(mesh_patch, extended, block_lists, block_counts):
    sample_realizations = mesh_patch.shape[0]
    analysis_block_count = mesh_patch.shape[2]
    tile_width = mesh_patch.shape[3]
    obs_ens = extended[:sample_realizations]
    obs_mean = lax.optimization_barrier(jnp.mean(obs_ens, axis=0))
    spread = obs_ens - obs_mean
    innovation = extended[sample_realizations] - obs_mean
    precision = extended[sample_realizations + 1]
    obs_row = extended[sample_realizations + 2]
    obs_col = extended[sample_realizations + 3]
    chosen = jnp.take(spread, block_lists, axis=1)
    active = (jnp.arange(block_lists.shape[1], dtype=jnp.int32)[None, :] < block_counts[:, None]).astype(jnp.float32)
    block_row = jnp.arange(analysis_block_count, dtype=jnp.float32)[:, None]
    row_gap = jnp.take(obs_row, block_lists) - block_row
    col_gap = jnp.take(obs_col, block_lists) - 0.5 * (tile_width - 1)
    tapering = jnp.exp(-0.5 * ((row_gap / LOC_ROWS) ** 2 + (col_gap / LOC_COLS) ** 2))
    weight = active * tapering * jnp.take(precision, block_lists)
    gram_matrix = jnp.einsum('erk,frk->ref', chosen * weight[None], chosen, precision=HIGHEST)
    forcing = jnp.einsum('erk,rk->re', chosen, weight * jnp.take(innovation, block_lists), precision=HIGHEST)
    identity = jnp.eye(sample_realizations, dtype=jnp.float32)
    system = (sample_realizations - 1.0) * identity + gram_matrix
    bounds = sample_realizations - 1.0 + lax.optimization_barrier(jnp.max(lax.optimization_barrier(jnp.sum(jnp.abs(gram_matrix), axis=2)), axis=1))
    upper_iter = system / bounds[:, None, None]
    lower_iter = jnp.broadcast_to(identity, system.shape)
    for iteration in range(NS_ITERS):
        factor = 1.5 * identity - 0.5 * jnp.einsum('rij,rjk->rik', lower_iter, upper_iter, precision=HIGHEST)
        upper_iter = jnp.einsum('rij,rjk->rik', upper_iter, factor, precision=HIGHEST)
        lower_iter = jnp.einsum('rij,rjk->rik', factor, lower_iter, precision=HIGHEST)
    inv_root = lower_iter / jnp.sqrt(bounds)[:, None, None]
    half_shift = jnp.einsum('rij,rj->ri', inv_root, forcing, precision=HIGHEST)
    mean_shift = jnp.einsum('rij,rj->ri', inv_root, half_shift, precision=HIGHEST)
    weights = jnp.sqrt(sample_realizations - 1.0) * inv_root + mean_shift[:, :, None]
    fields = mesh_patch.astype(jnp.float32)
    centre = lax.optimization_barrier(jnp.mean(fields, axis=0))
    anomalies = fields - centre
    updated = centre + jnp.einsum('kvrc,rkm->mvrc', anomalies, weights, precision=HIGHEST)
    return updated.astype(jnp.bfloat16)

def realization_predict(sample_states, wind_cfl_ratios):
    present_states = sample_states.astype(jnp.float32)
    diffusion = jnp.array(KAPPA, jnp.float32).reshape(2, 1, 1)
    for section_index in range(SECTIONS):
        padded = jnp.pad(present_states, ((0, 0), (1, 1), (0, 0)))
        present_states = advance(padded, wind_cfl_ratios[0], wind_cfl_ratios[1], diffusion)
    return present_states.astype(jnp.bfloat16)

def reference(prior_sample_states, wind_cfl_ratios, obs_cell, obs_value, obs_precision, neighbours, obs_counts):
    predict_advance = lax.map(lambda sample_states: realization_predict(sample_states, wind_cfl_ratios), prior_sample_states)
    sample_realizations = prior_sample_states.shape[0]
    quantity_leading = predict_advance[:, 0].reshape(sample_realizations, MESH_HEIGHT * MESH_WIDTH)
    cells = obs_cell.reshape(N_LAT, N_MEM, OBS_DEV)
    row_local = cells // PATCH_WIDTH
    col_local = cells % PATCH_WIDTH
    band_ids = jnp.arange(N_LAT, dtype=jnp.int32)[:, None, None]
    tile_ids = jnp.arange(N_MEM, dtype=jnp.int32)[None, :, None]
    flat_index = ((band_ids * ZONE_HEIGHT + row_local) * MESH_WIDTH + tile_ids * PATCH_WIDTH + col_local).astype(jnp.int32)
    sampled = jnp.take(quantity_leading, flat_index.reshape(-1), axis=1).astype(jnp.float32)
    sampled = jnp.transpose(sampled.reshape(sample_realizations, N_LAT, N_MEM, OBS_DEV), (1, 2, 0, 3))
    meta = jnp.stack([obs_value.reshape(N_LAT, N_MEM, OBS_DEV), obs_precision.reshape(N_LAT, N_MEM, OBS_DEV), row_local.astype(jnp.float32), col_local.astype(jnp.float32)], axis=2)
    combined = jnp.concatenate([sampled, meta], axis=2)
    padded = jnp.pad(combined, ((1, 1), (1, 1), (0, 0), (0, 0)))
    depth = sample_realizations + 4

    def fetch(zonal_strip, mesh_patch):
        return lax.dynamic_slice(padded, index_tuple(zonal_strip, mesh_patch, 0, 0), (1, 1, depth, OBS_DEV))[0, 0]

    def one_tile(index):
        zonal_strip = (index // N_MEM).astype(jnp.int32)
        mesh_patch = (index % N_MEM).astype(jnp.int32)
        pieces = [place_piece(fetch(zonal_strip + 1, mesh_patch + 1), sample_realizations, 0.0, 0.0), place_piece(fetch(zonal_strip, mesh_patch + 1), sample_realizations, -float(ZONE_HEIGHT), 0.0), place_piece(fetch(zonal_strip + 2, mesh_patch + 1), sample_realizations, float(ZONE_HEIGHT), 0.0), place_piece(fetch(zonal_strip + 1, mesh_patch), sample_realizations, 0.0, -float(PATCH_WIDTH)), place_piece(fetch(zonal_strip + 1, mesh_patch + 2), sample_realizations, 0.0, float(PATCH_WIDTH))]
        extended = jnp.concatenate(pieces, axis=1)
        states_by_patch = lax.dynamic_slice(predict_advance, index_tuple(0, 0, zonal_strip * ZONE_HEIGHT, mesh_patch * PATCH_WIDTH), (sample_realizations, 2, ZONE_HEIGHT, PATCH_WIDTH))
        block_lists = lax.dynamic_slice(neighbours, index_tuple(zonal_strip * ZONE_HEIGHT, mesh_patch, 0), (ZONE_HEIGHT, 1, KNB))[:, 0]
        block_counts = lax.dynamic_slice(obs_counts, index_tuple(zonal_strip * ZONE_HEIGHT, mesh_patch), (ZONE_HEIGHT, 1))[:, 0]
        return analyze(states_by_patch, extended, block_lists, block_counts)
    results = lax.map(one_tile, jnp.arange(N_LAT * N_MEM, dtype=jnp.int32))
    results = results.reshape(N_LAT, N_MEM, sample_realizations, 2, ZONE_HEIGHT, PATCH_WIDTH)
    return jnp.transpose(results, (2, 3, 0, 4, 1, 5)).reshape(sample_realizations, 2, MESH_HEIGHT, MESH_WIDTH)
```

```python
import functools
import math

import jax
import jax.numpy as jnp
from jax import lax
from jax.experimental import pallas as pl
from jax.experimental.pallas import tpu as pltpu
from jax.sharding import PartitionSpec as P

W = 128
SECTIONS = 4
NS_ITERS = 6
LOC_ROWS = 2
LOC_COLS = 64
KAPPA = (0.025, 0.0125)
HIGHEST = lax.Precision.HIGHEST
MESH = pl.DeviceIdType.MESH


def matmul(a, b, contract=((1,), (0,)), precision=None):
    return lax.dot_general(
        a, b, (contract, ((), ())), precision=precision, preferred_element_type=jnp.float32
    )


def hp(a, b, contract=((1,), (0,))):
    return matmul(a, b, contract, HIGHEST)


def kernel(
    n_mem, n_lat,
    prior_hbm, wind_hbm, cell_hbm, value_hbm, prec_hbm, nb_hbm, cnt_hbm,
    out_ref,
    prior, wind, cells, value, prec, nb, cnt, meta, packed, tiles, beside, moved,
    load_sem, halo_send, halo_recv, meta_send, meta_recv, tile_send, tile_recv, back_send, back_recv,
):
    f32, bf16, i32 = jnp.float32, jnp.bfloat16, jnp.int32
    u = lax.axis_index("mem")
    t = lax.axis_index("lat")
    members, _, rows, cols = prior_hbm.shape
    slots = nb_hbm.shape[2]
    n_obs = cell_hbm.shape[1]
    ens = members * n_mem
    big = ens * rows
    half = members * rows

    lat_up, lat_down = lax.rem(t + 1, n_lat), lax.rem(t + n_lat - 1, n_lat)
    mem_up, mem_down = lax.rem(u + 1, n_mem), lax.rem(u + n_mem - 1, n_mem)

    loads = [
        pltpu.make_async_copy(src, dst, load_sem.at[i])
        for i, (src, dst) in enumerate((
            (prior_hbm, prior.at[1]), (wind_hbm, wind.at[1]), (cell_hbm, cells), (value_hbm, value),
            (prec_hbm, prec), (nb_hbm, nb), (cnt_hbm, cnt),
        ))
    ]
    for load in loads:
        load.start()

    barrier = pltpu.get_barrier_semaphore()

    def greet(d, carry):
        for lat in (t, lat_up, lat_down):
            pl.semaphore_signal(
                barrier, inc=1, device_id={"mem": lax.rem(u + d, n_mem), "lat": lat}, device_id_type=MESH
            )
        return carry

    for lat in (lat_up, lat_down):
        pl.semaphore_signal(barrier, inc=1, device_id={"mem": u, "lat": lat}, device_id_type=MESH)
    lax.fori_loop(1, n_mem, greet, 0)
    pl.semaphore_wait(barrier, 3 * n_mem - 1)

    halos = []
    for side, lat in ((0, lat_up), (2, lat_down)):
        for kind, (src, dst) in enumerate(((prior_hbm, prior), (wind_hbm, wind))):
            copy = pltpu.make_async_remote_copy(
                src_ref=src, dst_ref=dst.at[side],
                send_sem=halo_send.at[side // 2, kind], recv_sem=halo_recv.at[side // 2, kind],
                device_id={"mem": u, "lat": lat}, device_id_type=MESH,
            )
            copy.start()
            halos.append(copy)

    for load in loads[2:]:
        load.wait()
    meta[0, 0:1, :] = cells[...].astype(f32)
    meta[0, 1:2, :] = value[...]
    meta[0, 2:3, :] = prec[...]
    meta[0, 3:8, :] = jnp.zeros((5, n_obs), f32)
    metas = []
    for slot, (mem, lat) in enumerate(((u, lat_up), (u, lat_down), (mem_up, t), (mem_down, t))):
        copy = pltpu.make_async_remote_copy(
            src_ref=meta.at[0], dst_ref=meta.at[slot + 1],
            send_sem=meta_send.at[slot], recv_sem=meta_recv.at[slot],
            device_id={"mem": mem, "lat": lat}, device_id_type=MESH,
        )
        copy.start()
        metas.append(copy)

    n_ext = 5 * n_obs
    n_hi = n_ext // W
    listed = jnp.concatenate([nb[r] for r in range(rows)], axis=1)
    counts = jnp.concatenate(
        [jnp.broadcast_to(cnt[r : r + 1, :], (1, slots)) for r in range(rows)], axis=1
    )
    position = lax.broadcasted_iota(i32, (1, rows * slots), 1)
    hi = lax.shift_right_logical(listed, 7)
    lo = lax.bitwise_and(listed, W - 1)
    hi = jnp.where(lax.bitwise_and(position, slots - 1) < counts, hi, n_hi + 8)
    sub = lax.broadcasted_iota(i32, (8 * n_hi, rows * slots), 0)
    owner = position // slots
    key = hi * 8 + owner
    left = (sub == key).astype(f32) + (sub == key + rows).astype(f32)
    right = (lax.broadcasted_iota(i32, (W, rows * slots), 0) == lo).astype(f32)
    member = matmul(left.astype(bf16), right.astype(bf16), ((1,), (1,)))
    member = jnp.concatenate([member[8 * h : 8 * h + 8] for h in range(n_hi)], axis=1)

    for load in loads[:2]:
        load.wait()
    for copy in halos:
        copy.wait()
    wide = 4 * rows
    row_id = lax.broadcasted_iota(i32, (wide, cols), 0)
    col_id = lax.broadcasted_iota(i32, (wide, cols), 1)
    first_row = jnp.where(t == 0, rows, 0)
    last_row = jnp.where(t == n_lat - 1, 2 * rows, 3 * rows)
    inside = (row_id >= first_row) & (row_id < last_row)

    def band(parts):
        return jnp.concatenate(list(parts) + [jnp.zeros((rows, cols), f32)], axis=0)

    east = band(wind[s, 0] for s in range(3))
    north = band(wind[s, 1] for s in range(3))
    east_pos, east_neg = jnp.maximum(east, 0.0), jnp.minimum(east, 0.0)
    north_pos, north_neg = jnp.maximum(north, 0.0), jnp.minimum(north, 0.0)
    fields = []
    for var in range(2):
        kappa = KAPPA[var]
        keep = jnp.where(inside, 1.0 - (east_pos - east_neg + north_pos - north_neg) - 4.0 * kappa, 0.0)
        from_west = jnp.where(inside & (col_id > 0), east_pos + kappa, 0.0)
        from_east = jnp.where(inside & (col_id < cols - 1), kappa - east_neg, 0.0)
        from_south = jnp.where(inside, north_pos + kappa, 0.0)
        from_north = jnp.where(inside, kappa - north_neg, 0.0)
        own = []
        for j in range(members):
            q = jnp.where(inside, band(prior[s, j, var].astype(f32) for s in range(3)), 0.0)
            for _ in range(SECTIONS):
                q = (
                    keep * q
                    + from_west * pltpu.roll(q, 1, 1)
                    + from_east * pltpu.roll(q, cols - 1, 1)
                    + from_south * pltpu.roll(q, 1, 0)
                    + from_north * pltpu.roll(q, wide - 1, 0)
                )
            own.append(q[rows : 2 * rows])
        fields.append(jnp.concatenate(own, axis=0).astype(bf16))
    for k in range(n_mem):
        for place, (var, tile) in enumerate(((0, (k - 1) % n_mem), (0, k), (0, (k + 1) % n_mem), (1, k))):
            packed[k, :, place * W : (place + 1) * W] = fields[var][:, tile * W : (tile + 1) * W]

    def beside_copy(mem, side, lat):
        return pltpu.make_async_remote_copy(
            src_ref=packed.at[mem, :, pl.ds(W, W)], dst_ref=beside.at[side, u],
            send_sem=tile_send.at[1 + side, mem], recv_sem=tile_recv.at[1 + side, u],
            device_id={"mem": mem, "lat": lat}, device_id_type=MESH,
        )

    def tile_copy(mem):
        return pltpu.make_async_remote_copy(
            src_ref=packed.at[mem], dst_ref=tiles.at[u],
            send_sem=tile_send.at[0, mem], recv_sem=tile_recv.at[0, u],
            device_id={"mem": mem, "lat": t}, device_id_type=MESH,
        )

    own_tile = pltpu.make_async_copy(packed.at[u], tiles.at[u], tile_recv.at[0, u])
    own_tile.start()

    def send_tiles(d, carry):
        mem = lax.rem(u + d, n_mem)
        tile_copy(mem).start()
        beside_copy(mem, 0, lat_up).start()
        beside_copy(mem, 1, lat_down).start()
        return carry

    lax.fori_loop(1, n_mem, send_tiles, 0)
    beside_copy(u, 0, lat_up).start()
    beside_copy(u, 1, lat_down).start()

    for copy in metas:
        copy.wait()
    cell = jnp.concatenate([meta[i, 0:1, :] for i in range(5)], axis=1)
    observed = jnp.concatenate([meta[i, 1:2, :] for i in range(5)], axis=1)
    valid = (None, t > 0, t < n_lat - 1, u > 0, u < n_mem - 1)
    precision = jnp.concatenate(
        [meta[0, 2:3, :]] + [jnp.where(valid[i], meta[i, 2:3, :], 0.0) for i in range(1, 5)], axis=1
    )
    cell_row = jnp.floor(cell * (1.0 / W))
    cell_col = cell - W * cell_row

    def spread_out(shifts):
        return jnp.concatenate([jnp.full((1, n_obs), s, f32) for s in shifts], axis=1)

    ext_row = cell_row + spread_out((0.0, -float(rows), float(rows), 0.0, 0.0))
    ext_col = cell_col + spread_out((0.0, 0.0, 0.0, -float(W), float(W)))
    block = lax.bitwise_and(lax.broadcasted_iota(i32, (8, n_ext), 0), rows - 1).astype(f32)
    row_gap = (ext_row - block) * (1.0 / LOC_ROWS)
    col_gap = (ext_col - 0.5 * (W - 1)) * (1.0 / LOC_COLS)
    weight = member * jnp.exp(-0.5 * (row_gap * row_gap + col_gap * col_gap)) * precision
    select = (lax.broadcasted_iota(i32, (W, n_ext), 0).astype(f32) == cell_col).astype(f32).astype(bf16)
    at_row = jnp.where(block == cell_row, 1.0, 0.0)
    ids0 = lax.broadcasted_iota(i32, (big, big), 0)
    ids1 = lax.broadcasted_iota(i32, (big, big), 1)
    same_member = (ids0 // rows == ids1 // rows).astype(f32).astype(bf16)
    same_block = lax.bitwise_and(ids0, rows - 1) == lax.bitwise_and(ids1, rows - 1)
    identity = (ids0 == ids1).astype(f32)

    own_tile.wait()

    def wait_tiles(d, carry):
        mem = lax.rem(u + d, n_mem)
        pltpu.make_async_copy(packed.at[0], tiles.at[mem], tile_recv.at[0, mem]).wait()
        return carry

    def wait_beside(mem, carry):
        for side in range(2):
            pltpu.make_async_copy(
                packed.at[0, :, pl.ds(W, W)], beside.at[side, mem], tile_recv.at[1 + side, mem]
            ).wait()
        return carry

    lax.fori_loop(1, n_mem, wait_tiles, 0)
    lax.fori_loop(0, n_mem, wait_beside, 0)

    states = tiles[...].astype(f32)

    def flat(x):
        return x.reshape(big, x.shape[-1])

    sources = (
        states[:, :, W : 2 * W], beside[0].astype(f32), beside[1].astype(f32),
        states[:, :, 0:W], states[:, :, 2 * W : 3 * W],
    )
    picked = jnp.concatenate(
        [
            matmul(flat(x).astype(bf16), select[:, i * n_obs : (i + 1) * n_obs])
            for i, x in enumerate(sources)
        ],
        axis=1,
    )
    picked = picked.reshape(n_mem, 8, n_ext) * at_row[None]
    obs = matmul(same_member, flat(picked).astype(bf16))
    obs3 = obs.reshape(n_mem, 8, n_ext)
    folded = jnp.sum(obs3, axis=0)
    obs_mean = jnp.sum(folded, axis=0, keepdims=True) * (1.0 / big)
    spread = obs - obs_mean
    innovation = observed - obs_mean
    weighted = flat(spread.reshape(n_mem, 8, n_ext) * weight[None])
    gram = jnp.where(same_block, hp(weighted, spread, ((1,), (1,))), 0.0)
    forcing = jnp.sum(weighted * innovation, axis=1, keepdims=True)

    def fold(x, op):
        folded = op(x.reshape(n_mem, 8, x.shape[-1]), axis=0)
        return folded

    row_sums = jnp.broadcast_to(jnp.sum(jnp.abs(gram), axis=1, keepdims=True), (big, W))
    top = jnp.max(row_sums.reshape(n_mem, 8, W), axis=0)
    top = jnp.maximum(top, pltpu.roll(top, rows, 0))
    bound = (ens - 1.0) + jnp.broadcast_to(top[None], (n_mem, 8, W)).reshape(big, W)[:, 0:1]
    upper = ((ens - 1.0) * identity + gram) / bound
    factor = 1.5 * identity - 0.5 * upper
    lower = factor
    upper = hp(upper, factor)
    for step in range(1, NS_ITERS):
        factor = 1.5 * identity - 0.5 * hp(lower, upper)
        if step < NS_ITERS - 1:
            upper = hp(upper, factor)
        lower = hp(factor, lower)
    root = lower / jnp.sqrt(bound)
    shift = hp(root, hp(root, jnp.broadcast_to(forcing, (big, W))))
    weights = math.sqrt(ens - 1.0) * root + jnp.where(same_block, shift[:, 0:1], 0.0)

    fields3 = jnp.concatenate([states[:, :, W : 2 * W], states[:, :, 3 * W : 4 * W]], axis=2)
    total = jnp.sum(fields3, axis=0)
    centre = (total + pltpu.roll(total, rows, 0)) * (1.0 / ens)
    anomalies = flat(fields3 - centre[None])
    updated = hp(weights, anomalies, ((0,), (0,))).reshape(n_mem, 8, 2 * W) + centre[None]
    for j in range(members):
        for var in range(2):
            moved[:, j, var] = updated[:, j * rows : (j + 1) * rows, var * W : (var + 1) * W].astype(bf16)

    def here(k):
        return out_ref.at[:, :, :, pl.ds(pl.multiple_of(k * W, W), W)]

    def back_copy(mem):
        return pltpu.make_async_remote_copy(
            src_ref=moved.at[mem], dst_ref=here(u),
            send_sem=back_send.at[mem], recv_sem=back_recv.at[u],
            device_id={"mem": mem, "lat": t}, device_id_type=MESH,
        )

    own_back = pltpu.make_async_copy(moved.at[u], here(u), back_recv.at[u])

    def send_back(d, carry):
        back_copy(lax.rem(u + d, n_mem)).start()
        return carry

    lax.fori_loop(1, n_mem, send_back, 0)
    own_back.start()

    def drain(d, carry):
        mem = lax.rem(u + d, n_mem)
        tile_copy(mem).wait_send()
        beside_copy(mem, 0, lat_up).wait_send()
        beside_copy(mem, 1, lat_down).wait_send()
        back_copy(mem).wait_send()
        return carry

    lax.fori_loop(1, n_mem, drain, 0)
    beside_copy(u, 0, lat_up).wait_send()
    beside_copy(u, 1, lat_down).wait_send()
    own_back.wait()

    def wait_back(d, carry):
        mem = lax.rem(u + d, n_mem)
        pltpu.make_async_copy(moved.at[mem], here(mem), back_recv.at[mem]).wait()
        return carry

    lax.fori_loop(1, n_mem, wait_back, 0)


def on_device(n_mem, n_lat, *args):
    prior, wind, cell, value, prec, nb, cnt = args
    members, _, rows, cols = prior.shape
    n_obs = cell.shape[1]
    f32, bf16, i32 = jnp.float32, jnp.bfloat16, jnp.int32
    dma = pltpu.SemaphoreType.DMA
    return pl.pallas_call(
        functools.partial(kernel, n_mem, n_lat),
        out_shape=jax.ShapeDtypeStruct(prior.shape, bf16),
        in_specs=[pl.BlockSpec(memory_space=pl.ANY)] * 7,
        out_specs=pl.BlockSpec(memory_space=pltpu.VMEM),
        scratch_shapes=[
            pltpu.VMEM((3,) + prior.shape, bf16),
            pltpu.VMEM((3,) + wind.shape, f32),
            pltpu.VMEM(cell.shape, i32),
            pltpu.VMEM(value.shape, f32),
            pltpu.VMEM(prec.shape, f32),
            pltpu.VMEM(nb.shape, i32),
            pltpu.VMEM(cnt.shape, i32),
            pltpu.VMEM((5, 8, n_obs), f32),
            pltpu.VMEM((n_mem, members * rows, 4 * W), bf16),
            pltpu.VMEM((n_mem, members * rows, 4 * W), bf16),
            pltpu.VMEM((2, n_mem, members * rows, W), bf16),
            pltpu.VMEM((n_mem, members, 2, rows, W), bf16),
            dma((7,)), dma((2, 2)), dma((2, 2)), dma((4,)), dma((4,)),
            dma((3, n_mem)), dma((3, n_mem)), dma((n_mem,)), dma((n_mem,)),
        ],
        compiler_params=pltpu.CompilerParams(collective_id=0, has_side_effects=True),
    )(prior, wind, cell, value, prec, nb, cnt)


def solution(mesh):
    placed = (
        P("mem", None, "lat", None),
        P(None, "lat", None),
        P("lat", "mem"),
        P("lat", "mem"),
        P("lat", "mem"),
        P("lat", "mem", None),
        P("lat", "mem"),
    )
    return jax.shard_map(
        functools.partial(on_device, mesh.shape["mem"], mesh.shape["lat"]),
        mesh=mesh,
        in_specs=placed,
        out_specs=P("mem", None, "lat", None),
        check_vma=False,
    )
```

```python
import functools
import math

import jax
import jax.numpy as jnp
from jax import lax
from jax.experimental import pallas as pl
from jax.experimental.pallas import tpu as pltpu
from jax.sharding import PartitionSpec as P

W = 128
SECTIONS = 4
NS_ITERS = 6
LOC_ROWS = 2
LOC_COLS = 64
KAPPA = (0.025, 0.0125)
MESH = pl.DeviceIdType.MESH


def matmul(a, b, contract=((1,), (0,))):
    return lax.dot_general(a, b, (contract, ((), ())), preferred_element_type=jnp.float32)


def halves(x):
    high = x.astype(jnp.bfloat16)
    return high, (x - high.astype(jnp.float32)).astype(jnp.bfloat16)


def hp(a, b, contract=((1,), (0,))):
    a_high, a_low = halves(a)
    b_high, b_low = halves(b)
    return matmul(a_high, b_high, contract) + (
        matmul(a_high, b_low, contract) + matmul(a_low, b_high, contract)
    )


def kernel(
    n_mem, n_lat,
    prior_hbm, wind_hbm, cell_hbm, value_hbm, prec_hbm, nb_hbm, cnt_hbm,
    out_ref,
    prior, wind, cells, value, prec, nb, cnt, meta, packed, tiles, beside, moved,
    load_sem, halo_send, halo_recv, meta_send, meta_recv, tile_send, tile_recv, back_send, back_recv, ready,
):
    f32, bf16, i32 = jnp.float32, jnp.bfloat16, jnp.int32
    u = lax.axis_index("mem")
    t = lax.axis_index("lat")
    members, _, rows, cols = prior_hbm.shape
    slots = nb_hbm.shape[2]
    n_obs = cell_hbm.shape[1]
    ens = members * n_mem
    big = ens * rows
    half = members * rows

    lat_up, lat_down, mem_up, mem_down = t + 1, t - 1, u + 1, u - 1
    above, below = t < n_lat - 1, t > 0
    east_of, west_of = u < n_mem - 1, u > 0
    lats = 1 + above.astype(i32) + below.astype(i32)

    def partner(k):
        up = k + (k >= u).astype(i32)
        k = n_mem - 1 - k
        return jnp.where(2 * u >= n_mem, up, k - (k <= u).astype(i32))

    def signal(sem, mem, lat):
        pl.semaphore_signal(sem, inc=1, device_id={"mem": mem, "lat": lat}, device_id_type=MESH)

    def signal_lats(sem, mem):
        signal(sem, mem, t)
        pl.when(above)(lambda: signal(sem, mem, lat_up))
        pl.when(below)(lambda: signal(sem, mem, lat_down))

    loads = [
        pltpu.make_async_copy(src, dst, load_sem.at[i])
        for i, (src, dst) in enumerate((
            (prior_hbm, prior.at[1]), (wind_hbm, wind.at[1]), (cell_hbm, cells), (value_hbm, value),
            (prec_hbm, prec), (nb_hbm, nb), (cnt_hbm, cnt),
        ))
    ]
    for load in loads:
        load.start()

    barrier = pltpu.get_barrier_semaphore()
    pl.when(above)(lambda: signal(barrier, u, lat_up))
    pl.when(below)(lambda: signal(barrier, u, lat_down))

    def greet(d, carry):
        signal_lats(barrier, n_mem - 1 - d)
        return carry

    lax.fori_loop(0, n_mem - 1 - u, greet, 0)
    pl.semaphore_wait(barrier, lats * (u + 1) - 1)

    def halo_copies(side, lat):
        return [
            pltpu.make_async_remote_copy(
                src_ref=src, dst_ref=dst.at[2 * side],
                send_sem=halo_send.at[side, kind], recv_sem=halo_recv.at[side, kind],
                device_id={"mem": u, "lat": lat}, device_id_type=MESH,
            )
            for kind, (src, dst) in enumerate(((prior_hbm, prior), (wind_hbm, wind)))
        ]

    def each(copies, act):
        for copy in copies:
            getattr(copy, act)()

    up_halo, down_halo = halo_copies(0, lat_up), halo_copies(1, lat_down)
    pl.when(above)(lambda: each(up_halo, "start"))
    pl.when(below)(lambda: each(down_halo, "start"))

    def answer(mem, carry):
        signal_lats(ready, mem)
        return carry

    lax.fori_loop(0, u, answer, 0)

    for load in loads[2:]:
        load.wait()
    meta[0, 0:1, :] = cells[...].astype(f32)
    meta[0, 1:2, :] = value[...]
    meta[0, 2:3, :] = prec[...]
    meta[0, 3:8, :] = jnp.zeros((5, n_obs), f32)
    metas = [
        pltpu.make_async_remote_copy(
            src_ref=meta.at[0], dst_ref=meta.at[slot + 1],
            send_sem=meta_send.at[slot], recv_sem=meta_recv.at[slot],
            device_id={"mem": mem, "lat": lat}, device_id_type=MESH,
        )
        for slot, (mem, lat) in enumerate(((u, lat_up), (u, lat_down), (mem_up, t), (mem_down, t)))
    ]
    meta_to = (above, below, east_of, west_of)
    meta_from = (below, above, west_of, east_of)

    def meta_zero(slot):
        meta[slot + 1] = jnp.zeros((8, n_obs), f32)

    for slot in (0, 1, 3):
        pl.when(meta_to[slot])(metas[slot].start)
    for slot in range(4):
        pl.when(jnp.logical_not(meta_from[slot]))(functools.partial(meta_zero, slot))

    n_ext = 5 * n_obs
    n_hi = n_ext // W
    listed = jnp.concatenate([nb[r] for r in range(rows)], axis=1)
    counts = jnp.concatenate(
        [jnp.broadcast_to(cnt[:, r : r + 1], (1, slots)) for r in range(rows)], axis=1
    )
    position = lax.broadcasted_iota(i32, (1, rows * slots), 1)
    hi = lax.shift_right_logical(listed, 7)
    lo = lax.bitwise_and(listed, W - 1)
    hi = jnp.where(lax.bitwise_and(position, slots - 1) < counts, hi, n_hi + 8)
    sub = lax.broadcasted_iota(i32, (8 * n_hi, rows * slots), 0)
    owner = position // slots
    key = hi * 8 + owner
    left = (sub == key).astype(f32) + (sub == key + rows).astype(f32)
    right = (lax.broadcasted_iota(i32, (W, rows * slots), 0) == lo).astype(f32)
    member = matmul(left.astype(bf16), right.astype(bf16), ((1,), (1,)))
    member = jnp.concatenate([member[8 * h : 8 * h + 8] for h in range(n_hi)], axis=1)

    for load in loads[:2]:
        load.wait()
    pl.when(below)(lambda: each(up_halo, "wait_recv"))
    pl.when(above)(lambda: each(down_halo, "wait_recv"))
    wide = 4 * rows
    row_id = lax.broadcasted_iota(i32, (wide, cols), 0)
    col_id = lax.broadcasted_iota(i32, (wide, cols), 1)
    first_row = jnp.where(t == 0, rows, 0)
    last_row = jnp.where(t == n_lat - 1, 2 * rows, 3 * rows)
    inside = (row_id >= first_row) & (row_id < last_row)

    def band(parts):
        return jnp.concatenate(list(parts) + [jnp.zeros((rows, cols), f32)], axis=0)

    east = band(wind[s, 0] for s in range(3))
    north = band(wind[s, 1] for s in range(3))
    east_pos, east_neg = jnp.maximum(east, 0.0), jnp.minimum(east, 0.0)
    north_pos, north_neg = jnp.maximum(north, 0.0), jnp.minimum(north, 0.0)
    fields = []
    for var in range(2):
        kappa = KAPPA[var]
        keep = jnp.where(inside, 1.0 - (east_pos - east_neg + north_pos - north_neg) - 4.0 * kappa, 0.0)
        from_west = jnp.where(inside & (col_id > 0), east_pos + kappa, 0.0)
        from_east = jnp.where(inside & (col_id < cols - 1), kappa - east_neg, 0.0)
        from_south = jnp.where(inside, north_pos + kappa, 0.0)
        from_north = jnp.where(inside, kappa - north_neg, 0.0)
        own = []
        for j in range(members):
            q = jnp.where(inside, band(prior[s, j, var].astype(f32) for s in range(3)), 0.0)
            for _ in range(SECTIONS):
                q = (
                    keep * q
                    + from_west * pltpu.roll(q, 1, 1)
                    + from_east * pltpu.roll(q, cols - 1, 1)
                    + from_south * pltpu.roll(q, 1, 0)
                    + from_north * pltpu.roll(q, wide - 1, 0)
                )
            own.append(q[rows : 2 * rows])
        fields.append(jnp.concatenate(own, axis=0).astype(bf16))
    for k in range(n_mem):
        for place, (var, tile) in enumerate(((0, (k - 1) % n_mem), (0, k), (0, (k + 1) % n_mem), (1, k))):
            packed[k, :, place * W : (place + 1) * W] = fields[var][:, tile * W : (tile + 1) * W]

    def beside_copy(mem, side, lat):
        return pltpu.make_async_remote_copy(
            src_ref=packed.at[mem, :, pl.ds(W, W)], dst_ref=beside.at[side, u],
            send_sem=tile_send.at[1 + side, mem], recv_sem=tile_recv.at[1 + side, u],
            device_id={"mem": mem, "lat": lat}, device_id_type=MESH,
        )

    def tile_copy(mem):
        return pltpu.make_async_remote_copy(
            src_ref=packed.at[mem], dst_ref=tiles.at[u],
            send_sem=tile_send.at[0, mem], recv_sem=tile_recv.at[0, u],
            device_id={"mem": mem, "lat": t}, device_id_type=MESH,
        )

    def beside_both(mem, act):
        pl.when(above)(lambda: getattr(beside_copy(mem, 0, lat_up), act)())
        pl.when(below)(lambda: getattr(beside_copy(mem, 1, lat_down), act)())

    pl.when(east_of)(lambda: pl.semaphore_wait(ready, lats * (n_mem - 1 - u)))
    pl.when(east_of)(metas[2].start)

    def send_tiles(k, carry):
        mem = partner(k)
        tile_copy(mem).start()
        beside_both(mem, "start")
        return carry

    lax.fori_loop(0, n_mem - 1, send_tiles, 0)
    beside_both(u, "start")
    own_tile = pltpu.make_async_copy(packed.at[u], tiles.at[u], tile_recv.at[0, u])
    own_tile.start()

    def beside_zero(side):
        beside[side] = jnp.zeros(beside.shape[1:], bf16)

    pl.when(jnp.logical_not(below))(lambda: beside_zero(0))
    pl.when(jnp.logical_not(above))(lambda: beside_zero(1))

    for slot in range(4):
        pl.when(meta_from[slot])(metas[slot].wait_recv)
    cell = jnp.concatenate([meta[i, 0:1, :] for i in range(5)], axis=1)
    observed = jnp.concatenate([meta[i, 1:2, :] for i in range(5)], axis=1)
    valid = (None,) + meta_from
    precision = jnp.concatenate(
        [meta[0, 2:3, :]] + [jnp.where(valid[i], meta[i, 2:3, :], 0.0) for i in range(1, 5)], axis=1
    )
    cell_row = jnp.floor(cell * (1.0 / W))
    cell_col = cell - W * cell_row

    def spread_out(shifts):
        return jnp.concatenate([jnp.full((1, n_obs), s, f32) for s in shifts], axis=1)

    ext_row = cell_row + spread_out((0.0, -float(rows), float(rows), 0.0, 0.0))
    ext_col = cell_col + spread_out((0.0, 0.0, 0.0, -float(W), float(W)))
    block = lax.bitwise_and(lax.broadcasted_iota(i32, (8, n_ext), 0), rows - 1).astype(f32)
    row_gap = (ext_row - block) * (1.0 / LOC_ROWS)
    col_gap = (ext_col - 0.5 * (W - 1)) * (1.0 / LOC_COLS)
    weight = member * jnp.exp(-0.5 * (row_gap * row_gap + col_gap * col_gap)) * precision
    select = (lax.broadcasted_iota(i32, (W, n_ext), 0).astype(f32) == cell_col).astype(f32).astype(bf16)
    at_row = jnp.where(block == cell_row, 1.0, 0.0)
    ids0 = lax.broadcasted_iota(i32, (big, big), 0)
    ids1 = lax.broadcasted_iota(i32, (big, big), 1)
    same_member = (ids0 // rows == ids1 // rows).astype(f32).astype(bf16)
    same_block = lax.bitwise_and(ids0, rows - 1) == lax.bitwise_and(ids1, rows - 1)
    identity = (ids0 == ids1).astype(f32)

    own_tile.wait()

    def wait_tiles(k, carry):
        mem = partner(k)
        pltpu.make_async_copy(packed.at[0], tiles.at[mem], tile_recv.at[0, mem]).wait()
        return carry

    def wait_beside(side):
        def wait_one(mem, carry):
            pltpu.make_async_copy(
                packed.at[0, :, pl.ds(W, W)], beside.at[side, mem], tile_recv.at[1 + side, mem]
            ).wait()
            return carry

        lax.fori_loop(0, n_mem, wait_one, 0)

    lax.fori_loop(0, n_mem - 1, wait_tiles, 0)
    pl.when(below)(lambda: wait_beside(0))
    pl.when(above)(lambda: wait_beside(1))

    states = tiles[...].astype(f32)

    def flat(x):
        return x.reshape(big, x.shape[-1])

    sources = (
        states[:, :, W : 2 * W], beside[0].astype(f32), beside[1].astype(f32),
        states[:, :, 0:W], states[:, :, 2 * W : 3 * W],
    )
    picked = jnp.concatenate(
        [
            matmul(flat(x).astype(bf16), select[:, i * n_obs : (i + 1) * n_obs])
            for i, x in enumerate(sources)
        ],
        axis=1,
    )
    picked = picked.reshape(n_mem, 8, n_ext) * at_row[None]
    obs = matmul(same_member, flat(picked).astype(bf16))
    obs3 = obs.reshape(n_mem, 8, n_ext)
    folded = jnp.sum(obs3, axis=0)
    obs_mean = jnp.sum(folded, axis=0, keepdims=True) * (1.0 / big)
    spread = obs - obs_mean
    innovation = observed - obs_mean
    weighted = flat(spread.reshape(n_mem, 8, n_ext) * weight[None])
    gram = jnp.where(same_block, hp(weighted, spread, ((1,), (1,))), 0.0)
    forcing = jnp.sum(weighted * innovation, axis=1, keepdims=True)

    fields3 = jnp.concatenate([states[:, :, W : 2 * W], states[:, :, 3 * W : 4 * W]], axis=2)
    total = jnp.sum(fields3, axis=0)
    centre = (total + pltpu.roll(total, rows, 0)) * (1.0 / ens)
    anomalies = flat(fields3 - centre[None])
    extra = jnp.concatenate([anomalies, jnp.broadcast_to(forcing, (big, W))], axis=1)

    row_sums = jnp.broadcast_to(jnp.sum(jnp.abs(gram), axis=1, keepdims=True), (big, W))
    top = jnp.max(row_sums.reshape(n_mem, 8, W), axis=0)
    top = jnp.maximum(top, pltpu.roll(top, rows, 0))
    bound = (ens - 1.0) + jnp.broadcast_to(top[None], (n_mem, 8, W)).reshape(big, W)[:, 0:1]
    upper = ((ens - 1.0) * identity + gram) / bound
    factor = 1.5 * identity - 0.5 * upper
    lower = factor
    upper = hp(upper, factor)
    for step in range(1, NS_ITERS):
        factor = 1.5 * identity - 0.5 * hp(lower, upper)
        if step < NS_ITERS - 1:
            upper = hp(upper, factor)
            lower = hp(factor, lower)
    rooted = hp(factor, hp(lower, extra)) / jnp.sqrt(bound)
    turned, half_shift = rooted[:, 0 : 2 * W], rooted[:, 2 * W : 2 * W + 1]
    shift = jnp.sum((turned * half_shift).reshape(n_mem, 8, 2 * W), axis=0)
    base = centre + shift + pltpu.roll(shift, rows, 0)
    updated = (math.sqrt(ens - 1.0) * turned).reshape(n_mem, 8, 2 * W) + base[None]
    for j in range(members):
        for var in range(2):
            moved[:, j, var] = updated[:, j * rows : (j + 1) * rows, var * W : (var + 1) * W].astype(bf16)

    def here(k):
        return out_ref.at[:, :, :, pl.ds(pl.multiple_of(k * W, W), W)]

    def back_copy(mem):
        return pltpu.make_async_remote_copy(
            src_ref=moved.at[mem], dst_ref=here(u),
            send_sem=back_send.at[mem], recv_sem=back_recv.at[u],
            device_id={"mem": mem, "lat": t}, device_id_type=MESH,
        )

    own_back = pltpu.make_async_copy(moved.at[u], here(u), back_recv.at[u])

    def send_back(k, carry):
        back_copy(partner(k)).start()
        return carry

    lax.fori_loop(0, n_mem - 1, send_back, 0)
    own_back.start()

    def drain(k, carry):
        mem = partner(k)
        tile_copy(mem).wait_send()
        beside_both(mem, "wait_send")
        return carry

    lax.fori_loop(0, n_mem - 1, drain, 0)
    beside_both(u, "wait_send")
    pl.when(above)(lambda: each(up_halo, "wait_send"))
    pl.when(below)(lambda: each(down_halo, "wait_send"))
    for slot in range(4):
        pl.when(meta_to[slot])(metas[slot].wait_send)
    own_back.wait()

    def wait_back(k, carry):
        mem = partner(k)
        back_copy(mem).wait_send()
        pltpu.make_async_copy(moved.at[mem], here(mem), back_recv.at[mem]).wait()
        return carry

    lax.fori_loop(0, n_mem - 1, wait_back, 0)


def on_device(n_mem, n_lat, *args):
    prior, wind, cell, value, prec, nb, cnt = args
    cnt = cnt.T
    members, _, rows, cols = prior.shape
    n_obs = cell.shape[1]
    f32, bf16, i32 = jnp.float32, jnp.bfloat16, jnp.int32
    dma = pltpu.SemaphoreType.DMA
    return pl.pallas_call(
        functools.partial(kernel, n_mem, n_lat),
        out_shape=jax.ShapeDtypeStruct(prior.shape, bf16),
        in_specs=[pl.BlockSpec(memory_space=pl.ANY)] * 7,
        out_specs=pl.BlockSpec(memory_space=pltpu.VMEM),
        scratch_shapes=[
            pltpu.VMEM((3,) + prior.shape, bf16),
            pltpu.VMEM((3,) + wind.shape, f32),
            pltpu.VMEM(cell.shape, i32),
            pltpu.VMEM(value.shape, f32),
            pltpu.VMEM(prec.shape, f32),
            pltpu.VMEM(nb.shape, i32),
            pltpu.VMEM(cnt.shape, i32),
            pltpu.VMEM((5, 8, n_obs), f32),
            pltpu.VMEM((n_mem, members * rows, 4 * W), bf16),
            pltpu.VMEM((n_mem, members * rows, 4 * W), bf16),
            pltpu.VMEM((2, n_mem, members * rows, W), bf16),
            pltpu.VMEM((n_mem, members, 2, rows, W), bf16),
            dma((7,)), dma((2, 2)), dma((2, 2)), dma((4,)), dma((4,)),
            dma((3, n_mem)), dma((3, n_mem)), dma((n_mem,)), dma((n_mem,)), pltpu.SemaphoreType.REGULAR,
        ],
        compiler_params=pltpu.CompilerParams(collective_id=0, has_side_effects=True),
    )(prior, wind, cell, value, prec, nb, cnt)


def solution(mesh):
    placed = (
        P("mem", None, "lat", None),
        P(None, "lat", None),
        P("lat", "mem"),
        P("lat", "mem"),
        P("lat", "mem"),
        P("lat", "mem", None),
        P("lat", "mem"),
    )
    return jax.shard_map(
        functools.partial(on_device, mesh.shape["mem"], mesh.shape["lat"]),
        mesh=mesh,
        in_specs=placed,
        out_specs=P("mem", None, "lat", None),
        check_vma=False,
    )
```

```python
import functools
import math

import jax
import jax.numpy as jnp
from jax import lax
from jax.experimental import pallas as pl
from jax.experimental.pallas import tpu as pltpu
from jax.sharding import PartitionSpec as P

W = 128
SECTIONS = 4
NS_ITERS = 6
LOC_ROWS = 2
LOC_COLS = 64
KAPPA = (0.025, 0.0125)
MESH = pl.DeviceIdType.MESH


def matmul(a, b, contract=((1,), (0,))):
    return lax.dot_general(a, b, (contract, ((), ())), preferred_element_type=jnp.float32)


def halves(x):
    high = x.astype(jnp.bfloat16)
    return high, (x - high.astype(jnp.float32)).astype(jnp.bfloat16)


def hp(a, b, contract=((1,), (0,))):
    a_high, a_low = halves(a)
    b_high, b_low = halves(b)
    return matmul(a_high, b_high, contract) + (
        matmul(a_high, b_low, contract) + matmul(a_low, b_high, contract)
    )


def kernel(
    n_mem, n_lat,
    prior_hbm, wind_hbm, cell_hbm, value_hbm, prec_hbm, nb_hbm, cnt_hbm,
    out_ref,
    prior, wind, cells, value, prec, nb, cnt, meta, packed, tiles, beside, moved,
    load_sem, halo_send, halo_recv, meta_send, meta_recv, tile_send, tile_recv, back_send, back_recv, ready,
):
    f32, bf16, i32 = jnp.float32, jnp.bfloat16, jnp.int32
    u = lax.axis_index("mem")
    t = lax.axis_index("lat")
    members, _, rows, cols = prior_hbm.shape
    slots = nb_hbm.shape[2]
    n_obs = cell_hbm.shape[1]
    ens = members * n_mem
    big = ens * rows
    half = members * rows

    lat_up, lat_down, mem_up, mem_down = t + 1, t - 1, u + 1, u - 1
    above, below = t < n_lat - 1, t > 0
    east_of, west_of = u < n_mem - 1, u > 0
    lats = 1 + above.astype(i32) + below.astype(i32)

    def partner(k):
        up = k + (k >= u).astype(i32)
        k = n_mem - 1 - k
        return jnp.where(2 * u >= n_mem, up, k - (k <= u).astype(i32))

    def signal(sem, mem, lat):
        pl.semaphore_signal(sem, inc=1, device_id={"mem": mem, "lat": lat}, device_id_type=MESH)

    def signal_lats(sem, mem):
        signal(sem, mem, t)
        pl.when(above)(lambda: signal(sem, mem, lat_up))
        pl.when(below)(lambda: signal(sem, mem, lat_down))

    loads = [
        pltpu.make_async_copy(src, dst, load_sem.at[i])
        for i, (src, dst) in enumerate((
            (prior_hbm, prior.at[1]), (wind_hbm, wind.at[1]), (cell_hbm, cells), (value_hbm, value),
            (prec_hbm, prec), (nb_hbm, nb), (cnt_hbm, cnt),
        ))
    ]
    for load in loads:
        load.start()

    barrier = pltpu.get_barrier_semaphore()
    pl.when(above)(lambda: signal(barrier, u, lat_up))
    pl.when(below)(lambda: signal(barrier, u, lat_down))

    def greet(d, carry):
        signal_lats(barrier, n_mem - 1 - d)
        return carry

    lax.fori_loop(0, n_mem - 1 - u, greet, 0)
    pl.semaphore_wait(barrier, lats * (u + 1) - 1)

    def halo_copies(side, lat):
        return [
            pltpu.make_async_remote_copy(
                src_ref=src, dst_ref=dst.at[2 * side],
                send_sem=halo_send.at[side, kind], recv_sem=halo_recv.at[side, kind],
                device_id={"mem": u, "lat": lat}, device_id_type=MESH,
            )
            for kind, (src, dst) in enumerate(((prior_hbm, prior), (wind_hbm, wind)))
        ]

    def each(copies, act):
        for copy in copies:
            getattr(copy, act)()

    up_halo, down_halo = halo_copies(0, lat_up), halo_copies(1, lat_down)
    pl.when(above)(lambda: each(up_halo, "start"))
    pl.when(below)(lambda: each(down_halo, "start"))

    def answer(mem, carry):
        signal_lats(ready, mem)
        return carry

    lax.fori_loop(0, u, answer, 0)

    for load in loads[2:]:
        load.wait()
    meta[0, 0:1, :] = cells[...].astype(f32)
    meta[0, 1:2, :] = value[...]
    meta[0, 2:3, :] = prec[...]
    meta[0, 3:8, :] = jnp.zeros((5, n_obs), f32)
    metas = [
        pltpu.make_async_remote_copy(
            src_ref=meta.at[0], dst_ref=meta.at[slot + 1],
            send_sem=meta_send.at[slot], recv_sem=meta_recv.at[slot],
            device_id={"mem": mem, "lat": lat}, device_id_type=MESH,
        )
        for slot, (mem, lat) in enumerate(((u, lat_up), (u, lat_down), (mem_up, t), (mem_down, t)))
    ]
    meta_to = (above, below, east_of, west_of)
    meta_from = (below, above, west_of, east_of)

    def meta_zero(slot):
        meta[slot + 1] = jnp.zeros((8, n_obs), f32)

    for slot in (0, 1, 3):
        pl.when(meta_to[slot])(metas[slot].start)
    for slot in range(4):
        pl.when(jnp.logical_not(meta_from[slot]))(functools.partial(meta_zero, slot))

    n_ext = 5 * n_obs
    n_hi = n_ext // W
    listed = jnp.concatenate([nb[r] for r in range(rows)], axis=1)
    counts = jnp.concatenate(
        [jnp.broadcast_to(cnt[:, r : r + 1], (1, slots)) for r in range(rows)], axis=1
    )
    position = lax.broadcasted_iota(i32, (1, rows * slots), 1)
    hi = lax.shift_right_logical(listed, 7)
    lo = lax.bitwise_and(listed, W - 1)
    hi = jnp.where(lax.bitwise_and(position, slots - 1) < counts, hi, n_hi + 8)
    sub = lax.broadcasted_iota(i32, (8 * n_hi, rows * slots), 0)
    owner = position // slots
    key = hi * 8 + owner
    left = (sub == key).astype(f32) + (sub == key + rows).astype(f32)
    right = (lax.broadcasted_iota(i32, (W, rows * slots), 0) == lo).astype(f32)
    member = matmul(left.astype(bf16), right.astype(bf16), ((1,), (1,)))
    member = jnp.concatenate([member[8 * h : 8 * h + 8] for h in range(n_hi)], axis=1)

    for load in loads[:2]:
        load.wait()
    pl.when(below)(lambda: each(up_halo, "wait_recv"))
    pl.when(above)(lambda: each(down_halo, "wait_recv"))
    wide = 4 * rows
    row_id = lax.broadcasted_iota(i32, (wide, cols), 0)
    col_id = lax.broadcasted_iota(i32, (wide, cols), 1)
    first_row = jnp.where(t == 0, rows, 0)
    last_row = jnp.where(t == n_lat - 1, 2 * rows, 3 * rows)
    inside = (row_id >= first_row) & (row_id < last_row)

    def band(parts):
        return jnp.concatenate(list(parts) + [jnp.zeros((rows, cols), f32)], axis=0)

    east = band(wind[s, 0] for s in range(3))
    north = band(wind[s, 1] for s in range(3))
    east_pos, east_neg = jnp.maximum(east, 0.0), jnp.minimum(east, 0.0)
    north_pos, north_neg = jnp.maximum(north, 0.0), jnp.minimum(north, 0.0)
    fields = []
    for var in range(2):
        kappa = KAPPA[var]
        keep = jnp.where(inside, 1.0 - (east_pos - east_neg + north_pos - north_neg) - 4.0 * kappa, 0.0)
        from_west = jnp.where(inside & (col_id > 0), east_pos + kappa, 0.0)
        from_east = jnp.where(inside & (col_id < cols - 1), kappa - east_neg, 0.0)
        from_south = jnp.where(inside, north_pos + kappa, 0.0)
        from_north = jnp.where(inside, kappa - north_neg, 0.0)
        own = []
        for j in range(members):
            q = jnp.where(inside, band(prior[s, j, var].astype(f32) for s in range(3)), 0.0)
            for _ in range(SECTIONS):
                q = (
                    keep * q
                    + from_west * pltpu.roll(q, 1, 1)
                    + from_east * pltpu.roll(q, cols - 1, 1)
                    + from_south * pltpu.roll(q, 1, 0)
                    + from_north * pltpu.roll(q, wide - 1, 0)
                )
            own.append(q[rows : 2 * rows])
        fields.append(jnp.concatenate(own, axis=0).astype(bf16))
    for k in range(n_mem):
        for place, (var, tile) in enumerate(((0, (k - 1) % n_mem), (0, k), (0, (k + 1) % n_mem), (1, k))):
            packed[k, :, place * W : (place + 1) * W] = fields[var][:, tile * W : (tile + 1) * W]

    def beside_copy(mem, side, lat):
        return pltpu.make_async_remote_copy(
            src_ref=packed.at[mem, :, pl.ds(W, W)], dst_ref=beside.at[side, u],
            send_sem=tile_send.at[1 + side, mem], recv_sem=tile_recv.at[1 + side, u],
            device_id={"mem": mem, "lat": lat}, device_id_type=MESH,
        )

    def tile_copy(mem):
        return pltpu.make_async_remote_copy(
            src_ref=packed.at[mem], dst_ref=tiles.at[u],
            send_sem=tile_send.at[0, mem], recv_sem=tile_recv.at[0, u],
            device_id={"mem": mem, "lat": t}, device_id_type=MESH,
        )

    def beside_both(mem, act):
        pl.when(above)(lambda: getattr(beside_copy(mem, 0, lat_up), act)())
        pl.when(below)(lambda: getattr(beside_copy(mem, 1, lat_down), act)())

    pl.when(east_of)(lambda: pl.semaphore_wait(ready, lats * (n_mem - 1 - u)))
    pl.when(east_of)(metas[2].start)

    def send_tiles(k, carry):
        mem = partner(k)
        tile_copy(mem).start()
        beside_both(mem, "start")
        return carry

    lax.fori_loop(0, n_mem - 1, send_tiles, 0)
    beside_both(u, "start")
    own_tile = pltpu.make_async_copy(packed.at[u], tiles.at[u], tile_recv.at[0, u])
    own_tile.start()

    def beside_zero(side):
        beside[side] = jnp.zeros(beside.shape[1:], bf16)

    pl.when(jnp.logical_not(below))(lambda: beside_zero(0))
    pl.when(jnp.logical_not(above))(lambda: beside_zero(1))

    for slot in range(4):
        pl.when(meta_from[slot])(metas[slot].wait_recv)
    cell = jnp.concatenate([meta[i, 0:1, :] for i in range(5)], axis=1)
    observed = jnp.concatenate([meta[i, 1:2, :] for i in range(5)], axis=1)
    valid = (None,) + meta_from
    precision = jnp.concatenate(
        [meta[0, 2:3, :]] + [jnp.where(valid[i], meta[i, 2:3, :], 0.0) for i in range(1, 5)], axis=1
    )
    cell_row = jnp.floor(cell * (1.0 / W))
    cell_col = cell - W * cell_row

    def spread_out(shifts):
        return jnp.concatenate([jnp.full((1, n_obs), s, f32) for s in shifts], axis=1)

    ext_row = cell_row + spread_out((0.0, -float(rows), float(rows), 0.0, 0.0))
    ext_col = cell_col + spread_out((0.0, 0.0, 0.0, -float(W), float(W)))
    block = lax.bitwise_and(lax.broadcasted_iota(i32, (8, n_ext), 0), rows - 1).astype(f32)
    row_gap = (ext_row - block) * (1.0 / LOC_ROWS)
    col_gap = (ext_col - 0.5 * (W - 1)) * (1.0 / LOC_COLS)
    weight = member * jnp.exp(-0.5 * (row_gap * row_gap + col_gap * col_gap)) * precision
    select = (lax.broadcasted_iota(i32, (W, n_ext), 0).astype(f32) == cell_col).astype(f32).astype(bf16)
    at_row = jnp.where(block == cell_row, 1.0, 0.0)
    ids0 = lax.broadcasted_iota(i32, (big, big), 0)
    ids1 = lax.broadcasted_iota(i32, (big, big), 1)
    same_member = (ids0 // rows == ids1 // rows).astype(f32).astype(bf16)
    same_block = lax.bitwise_and(ids0, rows - 1) == lax.bitwise_and(ids1, rows - 1)
    identity = (ids0 == ids1).astype(f32)

    own_tile.wait()

    def wait_tiles(k, carry):
        mem = partner(k)
        pltpu.make_async_copy(packed.at[0], tiles.at[mem], tile_recv.at[0, mem]).wait()
        return carry

    def wait_beside(side):
        def wait_one(mem, carry):
            pltpu.make_async_copy(
                packed.at[0, :, pl.ds(W, W)], beside.at[side, mem], tile_recv.at[1 + side, mem]
            ).wait()
            return carry

        lax.fori_loop(0, n_mem, wait_one, 0)

    lax.fori_loop(0, n_mem - 1, wait_tiles, 0)
    pl.when(below)(lambda: wait_beside(0))
    pl.when(above)(lambda: wait_beside(1))

    states = tiles[...].astype(f32)

    def flat(x):
        return x.reshape(big, x.shape[-1])

    sources = (
        states[:, :, W : 2 * W], beside[0].astype(f32), beside[1].astype(f32),
        states[:, :, 0:W], states[:, :, 2 * W : 3 * W],
    )
    picked = jnp.concatenate(
        [
            matmul(flat(x).astype(bf16), select[:, i * n_obs : (i + 1) * n_obs])
            for i, x in enumerate(sources)
        ],
        axis=1,
    )
    picked = picked.reshape(n_mem, 8, n_ext) * at_row[None]
    obs = matmul(same_member, flat(picked).astype(bf16))
    obs3 = obs.reshape(n_mem, 8, n_ext)
    folded = jnp.sum(obs3, axis=0)
    obs_mean = jnp.sum(folded, axis=0, keepdims=True) * (1.0 / big)
    spread = obs - obs_mean
    innovation = observed - obs_mean
    weighted = flat(spread.reshape(n_mem, 8, n_ext) * weight[None])
    gram = jnp.where(same_block, hp(weighted, spread, ((1,), (1,))), 0.0)
    forcing = jnp.sum(weighted * innovation, axis=1, keepdims=True)

    fields3 = jnp.concatenate([states[:, :, W : 2 * W], states[:, :, 3 * W : 4 * W]], axis=2)
    total = jnp.sum(fields3, axis=0)
    centre = (total + pltpu.roll(total, rows, 0)) * (1.0 / ens)
    anomalies = flat(fields3 - centre[None])
    extra = jnp.concatenate([anomalies, jnp.broadcast_to(forcing, (big, W))], axis=1)

    row_sums = jnp.broadcast_to(jnp.sum(jnp.abs(gram), axis=1, keepdims=True), (big, W))
    top = jnp.max(row_sums.reshape(n_mem, 8, W), axis=0)
    top = jnp.maximum(top, pltpu.roll(top, rows, 0))
    bound = (ens - 1.0) + jnp.broadcast_to(top[None], (n_mem, 8, W)).reshape(big, W)[:, 0:1]
    upper = ((ens - 1.0) * identity + gram) / bound
    factor = 1.5 * identity - 0.5 * upper
    lower = factor
    upper = hp(upper, factor)
    for step in range(1, NS_ITERS):
        factor = 1.5 * identity - 0.5 * hp(lower, upper)
        if step < NS_ITERS - 1:
            upper = hp(upper, factor)
            lower = hp(factor, lower)
    rooted = hp(factor, hp(lower, extra)) / jnp.sqrt(bound)
    turned, half_shift = rooted[:, 0 : 2 * W], rooted[:, 2 * W : 2 * W + 1]
    shift = jnp.sum((turned * half_shift).reshape(n_mem, 8, 2 * W), axis=0)
    base = centre + shift + pltpu.roll(shift, rows, 0)
    updated = (math.sqrt(ens - 1.0) * turned).reshape(n_mem, 8, 2 * W) + base[None]
    for j in range(members):
        for var in range(2):
            moved[:, j, var] = updated[:, j * rows : (j + 1) * rows, var * W : (var + 1) * W].astype(bf16)

    def here(k):
        return out_ref.at[:, :, :, pl.ds(pl.multiple_of(k * W, W), W)]

    def back_copy(mem):
        return pltpu.make_async_remote_copy(
            src_ref=moved.at[mem], dst_ref=here(u),
            send_sem=back_send.at[mem], recv_sem=back_recv.at[u],
            device_id={"mem": mem, "lat": t}, device_id_type=MESH,
        )

    own_back = pltpu.make_async_copy(moved.at[u], here(u), back_recv.at[u])

    def send_back(k, carry):
        back_copy(partner(k)).start()
        return carry

    lax.fori_loop(0, n_mem - 1, send_back, 0)
    own_back.start()

    def drain(k, carry):
        mem = partner(k)
        tile_copy(mem).wait_send()
        beside_both(mem, "wait_send")
        return carry

    lax.fori_loop(0, n_mem - 1, drain, 0)
    beside_both(u, "wait_send")
    pl.when(above)(lambda: each(up_halo, "wait_send"))
    pl.when(below)(lambda: each(down_halo, "wait_send"))
    for slot in range(4):
        pl.when(meta_to[slot])(metas[slot].wait_send)
    own_back.wait()

    def wait_back(k, carry):
        mem = partner(k)
        back_copy(mem).wait_send()
        pltpu.make_async_copy(moved.at[mem], here(mem), back_recv.at[mem]).wait()
        return carry

    lax.fori_loop(0, n_mem - 1, wait_back, 0)


def on_device(n_mem, n_lat, *args):
    prior, wind, cell, value, prec, nb, cnt = args
    cnt = cnt.T
    members, _, rows, cols = prior.shape
    n_obs = cell.shape[1]
    f32, bf16, i32 = jnp.float32, jnp.bfloat16, jnp.int32
    dma = pltpu.SemaphoreType.DMA
    return pl.pallas_call(
        functools.partial(kernel, n_mem, n_lat),
        out_shape=pltpu.VMEM(prior.shape, bf16),
        in_specs=[pl.BlockSpec(memory_space=pl.ANY)] * 7,
        out_specs=pl.BlockSpec(memory_space=pltpu.VMEM),
        scratch_shapes=[
            pltpu.VMEM((3,) + prior.shape, bf16),
            pltpu.VMEM((3,) + wind.shape, f32),
            pltpu.VMEM(cell.shape, i32),
            pltpu.VMEM(value.shape, f32),
            pltpu.VMEM(prec.shape, f32),
            pltpu.VMEM(nb.shape, i32),
            pltpu.VMEM(cnt.shape, i32),
            pltpu.VMEM((5, 8, n_obs), f32),
            pltpu.VMEM((n_mem, members * rows, 4 * W), bf16),
            pltpu.VMEM((n_mem, members * rows, 4 * W), bf16),
            pltpu.VMEM((2, n_mem, members * rows, W), bf16),
            pltpu.VMEM((n_mem, members, 2, rows, W), bf16),
            dma((7,)), dma((2, 2)), dma((2, 2)), dma((4,)), dma((4,)),
            dma((3, n_mem)), dma((3, n_mem)), dma((n_mem,)), dma((n_mem,)), pltpu.SemaphoreType.REGULAR,
        ],
        compiler_params=pltpu.CompilerParams(collective_id=0, has_side_effects=True),
    )(prior, wind, cell, value, prec, nb, cnt)


def solution(mesh):
    placed = (
        P("mem", None, "lat", None),
        P(None, "lat", None),
        P("lat", "mem"),
        P("lat", "mem"),
        P("lat", "mem"),
        P("lat", "mem", None),
        P("lat", "mem"),
    )
    return jax.shard_map(
        functools.partial(on_device, mesh.shape["mem"], mesh.shape["lat"]),
        mesh=mesh,
        in_specs=placed,
        out_specs=P("mem", None, "lat", None),
        check_vma=False,
    )
```

```python
import functools
import math

import jax
import jax.numpy as jnp
from jax import lax
from jax.experimental import pallas as pl
from jax.experimental.pallas import tpu as pltpu
from jax.sharding import PartitionSpec as P

W = 128
SECTIONS = 4
NS_ITERS = 6
LOC_ROWS = 2
LOC_COLS = 64
KAPPA = (0.025, 0.0125)
MESH = pl.DeviceIdType.MESH


def matmul(a, b, contract=((1,), (0,))):
    return lax.dot_general(a, b, (contract, ((), ())), preferred_element_type=jnp.float32)


def halves(x):
    high = x.astype(jnp.bfloat16)
    return high, (x - high.astype(jnp.float32)).astype(jnp.bfloat16)


def hp(a, b, contract=((1,), (0,))):
    a_high, a_low = halves(a)
    b_high, b_low = halves(b)
    return matmul(a_high, b_high, contract) + (
        matmul(a_high, b_low, contract) + matmul(a_low, b_high, contract)
    )


def kernel(
    n_mem, n_lat,
    prior_hbm, wind_hbm, cell_hbm, value_hbm, prec_hbm, nb_hbm, cnt_hbm,
    out_ref,
    prior, wind, cells, value, prec, nb, cnt, meta, packed, tiles, beside, moved,
    load_sem, halo_send, halo_recv, meta_send, meta_recv, tile_send, tile_recv, back_send, back_recv, ready,
):
    f32, bf16, i32 = jnp.float32, jnp.bfloat16, jnp.int32
    u = lax.axis_index("mem")
    t = lax.axis_index("lat")
    members, _, rows, cols = prior_hbm.shape
    slots = nb_hbm.shape[2]
    n_obs = cell_hbm.shape[1]
    ens = members * n_mem
    big = ens * rows
    half = members * rows

    lat_up, lat_down, mem_up, mem_down = t + 1, t - 1, u + 1, u - 1
    above, below = t < n_lat - 1, t > 0
    east_of, west_of = u < n_mem - 1, u > 0
    lats = 1 + above.astype(i32) + below.astype(i32)

    def partner(k):
        up = k + (k >= u).astype(i32)
        k = n_mem - 1 - k
        return jnp.where(2 * u >= n_mem, up, k - (k <= u).astype(i32))

    def signal(sem, mem, lat):
        pl.semaphore_signal(sem, inc=1, device_id={"mem": mem, "lat": lat}, device_id_type=MESH)

    def signal_lats(sem, mem):
        signal(sem, mem, t)
        pl.when(above)(lambda: signal(sem, mem, lat_up))
        pl.when(below)(lambda: signal(sem, mem, lat_down))

    loads = [
        pltpu.make_async_copy(src, dst, load_sem.at[i])
        for i, (src, dst) in enumerate((
            (prior_hbm, prior.at[1]), (wind_hbm, wind.at[1]), (cell_hbm, cells), (value_hbm, value),
            (prec_hbm, prec), (nb_hbm, nb), (cnt_hbm, cnt),
        ))
    ]
    for load in loads:
        load.start()

    barrier = pltpu.get_barrier_semaphore()
    pl.when(above)(lambda: signal(barrier, u, lat_up))
    pl.when(below)(lambda: signal(barrier, u, lat_down))

    def greet(d, carry):
        signal_lats(barrier, n_mem - 1 - d)
        return carry

    lax.fori_loop(0, n_mem - 1 - u, greet, 0)
    pl.semaphore_wait(barrier, lats * (u + 1) - 1)
    for load in loads[:2]:
        load.wait()

    def halo_copies(side, lat):
        return [
            pltpu.make_async_remote_copy(
                src_ref=src, dst_ref=dst.at[2 * side],
                send_sem=halo_send.at[side, kind], recv_sem=halo_recv.at[side, kind],
                device_id={"mem": u, "lat": lat}, device_id_type=MESH,
            )
            for kind, (src, dst) in enumerate(((prior.at[1], prior), (wind.at[1], wind)))
        ]

    def each(copies, act):
        for copy in copies:
            getattr(copy, act)()

    up_halo, down_halo = halo_copies(0, lat_up), halo_copies(1, lat_down)
    pl.when(above)(lambda: each(up_halo, "start"))
    pl.when(below)(lambda: each(down_halo, "start"))

    def answer(mem, carry):
        signal_lats(ready, mem)
        return carry

    lax.fori_loop(0, u, answer, 0)

    for load in loads[2:]:
        load.wait()
    meta[0, 0:1, :] = cells[...].astype(f32)
    meta[0, 1:2, :] = value[...]
    meta[0, 2:3, :] = prec[...]
    meta[0, 3:8, :] = jnp.zeros((5, n_obs), f32)
    metas = [
        pltpu.make_async_remote_copy(
            src_ref=meta.at[0], dst_ref=meta.at[slot + 1],
            send_sem=meta_send.at[slot], recv_sem=meta_recv.at[slot],
            device_id={"mem": mem, "lat": lat}, device_id_type=MESH,
        )
        for slot, (mem, lat) in enumerate(((u, lat_up), (u, lat_down), (mem_up, t), (mem_down, t)))
    ]
    meta_to = (above, below, east_of, west_of)
    meta_from = (below, above, west_of, east_of)

    def meta_zero(slot):
        meta[slot + 1] = jnp.zeros((8, n_obs), f32)

    for slot in (0, 1, 3):
        pl.when(meta_to[slot])(metas[slot].start)
    for slot in range(4):
        pl.when(jnp.logical_not(meta_from[slot]))(functools.partial(meta_zero, slot))

    n_ext = 5 * n_obs
    n_hi = n_ext // W
    listed = jnp.concatenate([nb[r] for r in range(rows)], axis=1)
    counts = jnp.concatenate(
        [jnp.broadcast_to(cnt[:, r : r + 1], (1, slots)) for r in range(rows)], axis=1
    )
    position = lax.broadcasted_iota(i32, (1, rows * slots), 1)
    hi = lax.shift_right_logical(listed, 7)
    lo = lax.bitwise_and(listed, W - 1)
    hi = jnp.where(lax.bitwise_and(position, slots - 1) < counts, hi, n_hi + 8)
    sub = lax.broadcasted_iota(i32, (8 * n_hi, rows * slots), 0)
    owner = position // slots
    key = hi * 8 + owner
    left = (sub == key).astype(f32) + (sub == key + rows).astype(f32)
    right = (lax.broadcasted_iota(i32, (W, rows * slots), 0) == lo).astype(f32)
    member = matmul(left.astype(bf16), right.astype(bf16), ((1,), (1,)))
    member = jnp.concatenate([member[8 * h : 8 * h + 8] for h in range(n_hi)], axis=1)

    pl.when(below)(lambda: each(up_halo, "wait_recv"))
    pl.when(above)(lambda: each(down_halo, "wait_recv"))
    wide = 4 * rows
    row_id = lax.broadcasted_iota(i32, (wide, cols), 0)
    col_id = lax.broadcasted_iota(i32, (wide, cols), 1)
    first_row = jnp.where(t == 0, rows, 0)
    last_row = jnp.where(t == n_lat - 1, 2 * rows, 3 * rows)
    inside = (row_id >= first_row) & (row_id < last_row)

    def band(parts):
        return jnp.concatenate(list(parts) + [jnp.zeros((rows, cols), f32)], axis=0)

    east = band(wind[s, 0] for s in range(3))
    north = band(wind[s, 1] for s in range(3))
    east_pos, east_neg = jnp.maximum(east, 0.0), jnp.minimum(east, 0.0)
    north_pos, north_neg = jnp.maximum(north, 0.0), jnp.minimum(north, 0.0)
    fields = []
    for var in range(2):
        kappa = KAPPA[var]
        keep = jnp.where(inside, 1.0 - (east_pos - east_neg + north_pos - north_neg) - 4.0 * kappa, 0.0)
        from_west = jnp.where(inside & (col_id > 0), east_pos + kappa, 0.0)
        from_east = jnp.where(inside & (col_id < cols - 1), kappa - east_neg, 0.0)
        from_south = jnp.where(inside, north_pos + kappa, 0.0)
        from_north = jnp.where(inside, kappa - north_neg, 0.0)
        own = []
        for j in range(members):
            q = jnp.where(inside, band(prior[s, j, var].astype(f32) for s in range(3)), 0.0)
            for _ in range(SECTIONS):
                q = (
                    keep * q
                    + from_west * pltpu.roll(q, 1, 1)
                    + from_east * pltpu.roll(q, cols - 1, 1)
                    + from_south * pltpu.roll(q, 1, 0)
                    + from_north * pltpu.roll(q, wide - 1, 0)
                )
            own.append(q[rows : 2 * rows])
        fields.append(jnp.concatenate(own, axis=0).astype(bf16))
    for k in range(n_mem):
        for place, (var, tile) in enumerate(((0, (k - 1) % n_mem), (0, k), (0, (k + 1) % n_mem), (1, k))):
            packed[k, :, place * W : (place + 1) * W] = fields[var][:, tile * W : (tile + 1) * W]

    def beside_copy(mem, side, lat):
        return pltpu.make_async_remote_copy(
            src_ref=packed.at[mem, :, pl.ds(W, W)], dst_ref=beside.at[side, u],
            send_sem=tile_send.at[1 + side, mem], recv_sem=tile_recv.at[1 + side, u],
            device_id={"mem": mem, "lat": lat}, device_id_type=MESH,
        )

    def tile_copy(mem):
        return pltpu.make_async_remote_copy(
            src_ref=packed.at[mem], dst_ref=tiles.at[u],
            send_sem=tile_send.at[0, mem], recv_sem=tile_recv.at[0, u],
            device_id={"mem": mem, "lat": t}, device_id_type=MESH,
        )

    def beside_both(mem, act):
        pl.when(above)(lambda: getattr(beside_copy(mem, 0, lat_up), act)())
        pl.when(below)(lambda: getattr(beside_copy(mem, 1, lat_down), act)())

    pl.when(east_of)(lambda: pl.semaphore_wait(ready, lats * (n_mem - 1 - u)))
    pl.when(east_of)(metas[2].start)

    def send_tiles(k, carry):
        mem = partner(k)
        tile_copy(mem).start()
        beside_both(mem, "start")
        return carry

    lax.fori_loop(0, n_mem - 1, send_tiles, 0)
    beside_both(u, "start")
    own_tile = pltpu.make_async_copy(packed.at[u], tiles.at[u], tile_recv.at[0, u])
    own_tile.start()

    def beside_zero(side):
        beside[side] = jnp.zeros(beside.shape[1:], bf16)

    pl.when(jnp.logical_not(below))(lambda: beside_zero(0))
    pl.when(jnp.logical_not(above))(lambda: beside_zero(1))

    for slot in range(4):
        pl.when(meta_from[slot])(metas[slot].wait_recv)
    cell = jnp.concatenate([meta[i, 0:1, :] for i in range(5)], axis=1)
    observed = jnp.concatenate([meta[i, 1:2, :] for i in range(5)], axis=1)
    valid = (None,) + meta_from
    precision = jnp.concatenate(
        [meta[0, 2:3, :]] + [jnp.where(valid[i], meta[i, 2:3, :], 0.0) for i in range(1, 5)], axis=1
    )
    cell_row = jnp.floor(cell * (1.0 / W))
    cell_col = cell - W * cell_row

    def spread_out(shifts):
        return jnp.concatenate([jnp.full((1, n_obs), s, f32) for s in shifts], axis=1)

    ext_row = cell_row + spread_out((0.0, -float(rows), float(rows), 0.0, 0.0))
    ext_col = cell_col + spread_out((0.0, 0.0, 0.0, -float(W), float(W)))
    block = lax.bitwise_and(lax.broadcasted_iota(i32, (8, n_ext), 0), rows - 1).astype(f32)
    row_gap = (ext_row - block) * (1.0 / LOC_ROWS)
    col_gap = (ext_col - 0.5 * (W - 1)) * (1.0 / LOC_COLS)
    weight = member * jnp.exp(-0.5 * (row_gap * row_gap + col_gap * col_gap)) * precision
    select = (lax.broadcasted_iota(i32, (W, n_ext), 0).astype(f32) == cell_col).astype(f32).astype(bf16)
    at_row = jnp.where(block == cell_row, 1.0, 0.0)
    ids0 = lax.broadcasted_iota(i32, (big, big), 0)
    ids1 = lax.broadcasted_iota(i32, (big, big), 1)
    same_member = (ids0 // rows == ids1 // rows).astype(f32).astype(bf16)
    same_block = lax.bitwise_and(ids0, rows - 1) == lax.bitwise_and(ids1, rows - 1)
    identity = (ids0 == ids1).astype(f32)

    own_tile.wait()

    def wait_tiles(k, carry):
        mem = partner(k)
        pltpu.make_async_copy(packed.at[0], tiles.at[mem], tile_recv.at[0, mem]).wait()
        return carry

    def wait_beside(side):
        def wait_one(mem, carry):
            pltpu.make_async_copy(
                packed.at[0, :, pl.ds(W, W)], beside.at[side, mem], tile_recv.at[1 + side, mem]
            ).wait()
            return carry

        lax.fori_loop(0, n_mem, wait_one, 0)

    lax.fori_loop(0, n_mem - 1, wait_tiles, 0)
    pl.when(below)(lambda: wait_beside(0))
    pl.when(above)(lambda: wait_beside(1))

    states = tiles[...].astype(f32)

    def flat(x):
        return x.reshape(big, x.shape[-1])

    sources = (
        states[:, :, W : 2 * W], beside[0].astype(f32), beside[1].astype(f32),
        states[:, :, 0:W], states[:, :, 2 * W : 3 * W],
    )
    picked = jnp.concatenate(
        [
            matmul(flat(x).astype(bf16), select[:, i * n_obs : (i + 1) * n_obs])
            for i, x in enumerate(sources)
        ],
        axis=1,
    )
    picked = picked.reshape(n_mem, 8, n_ext) * at_row[None]
    obs = matmul(same_member, flat(picked).astype(bf16))
    obs3 = obs.reshape(n_mem, 8, n_ext)
    folded = jnp.sum(obs3, axis=0)
    obs_mean = jnp.sum(folded, axis=0, keepdims=True) * (1.0 / big)
    spread = obs - obs_mean
    innovation = observed - obs_mean
    weighted = flat(spread.reshape(n_mem, 8, n_ext) * weight[None])
    gram = jnp.where(same_block, hp(weighted, spread, ((1,), (1,))), 0.0)
    forcing = jnp.sum(weighted * innovation, axis=1, keepdims=True)

    fields3 = jnp.concatenate([states[:, :, W : 2 * W], states[:, :, 3 * W : 4 * W]], axis=2)
    total = jnp.sum(fields3, axis=0)
    centre = (total + pltpu.roll(total, rows, 0)) * (1.0 / ens)
    anomalies = flat(fields3 - centre[None])
    extra = jnp.concatenate([anomalies, jnp.broadcast_to(forcing, (big, W))], axis=1)

    row_sums = jnp.broadcast_to(jnp.sum(jnp.abs(gram), axis=1, keepdims=True), (big, W))
    top = jnp.max(row_sums.reshape(n_mem, 8, W), axis=0)
    top = jnp.maximum(top, pltpu.roll(top, rows, 0))
    bound = (ens - 1.0) + jnp.broadcast_to(top[None], (n_mem, 8, W)).reshape(big, W)[:, 0:1]
    upper = ((ens - 1.0) * identity + gram) / bound
    factor = 1.5 * identity - 0.5 * upper
    lower = factor
    upper = hp(upper, factor)
    for step in range(1, NS_ITERS):
        factor = 1.5 * identity - 0.5 * hp(lower, upper)
        if step < NS_ITERS - 1:
            upper = hp(upper, factor)
            lower = hp(factor, lower)
    rooted = hp(factor, hp(lower, extra)) / jnp.sqrt(bound)
    turned, half_shift = rooted[:, 0 : 2 * W], rooted[:, 2 * W : 2 * W + 1]
    shift = jnp.sum((turned * half_shift).reshape(n_mem, 8, 2 * W), axis=0)
    base = centre + shift + pltpu.roll(shift, rows, 0)
    updated = (math.sqrt(ens - 1.0) * turned).reshape(n_mem, 8, 2 * W) + base[None]
    for j in range(members):
        for var in range(2):
            moved[:, j, var] = updated[:, j * rows : (j + 1) * rows, var * W : (var + 1) * W].astype(bf16)

    def here(k):
        return out_ref.at[:, :, :, pl.ds(pl.multiple_of(k * W, W), W)]

    def back_copy(mem):
        return pltpu.make_async_remote_copy(
            src_ref=moved.at[mem], dst_ref=here(u),
            send_sem=back_send.at[mem], recv_sem=back_recv.at[u],
            device_id={"mem": mem, "lat": t}, device_id_type=MESH,
        )

    own_back = pltpu.make_async_copy(moved.at[u], here(u), back_recv.at[u])

    def send_back(k, carry):
        back_copy(partner(k)).start()
        return carry

    lax.fori_loop(0, n_mem - 1, send_back, 0)
    own_back.start()

    def drain(k, carry):
        mem = partner(k)
        tile_copy(mem).wait_send()
        beside_both(mem, "wait_send")
        return carry

    lax.fori_loop(0, n_mem - 1, drain, 0)
    beside_both(u, "wait_send")
    pl.when(above)(lambda: each(up_halo, "wait_send"))
    pl.when(below)(lambda: each(down_halo, "wait_send"))
    for slot in range(4):
        pl.when(meta_to[slot])(metas[slot].wait_send)
    own_back.wait()

    def wait_back(k, carry):
        mem = partner(k)
        back_copy(mem).wait_send()
        pltpu.make_async_copy(moved.at[mem], here(mem), back_recv.at[mem]).wait()
        return carry

    lax.fori_loop(0, n_mem - 1, wait_back, 0)


def on_device(n_mem, n_lat, *args):
    prior, wind, cell, value, prec, nb, cnt = args
    cnt = cnt.T
    members, _, rows, cols = prior.shape
    n_obs = cell.shape[1]
    f32, bf16, i32 = jnp.float32, jnp.bfloat16, jnp.int32
    dma = pltpu.SemaphoreType.DMA
    return pl.pallas_call(
        functools.partial(kernel, n_mem, n_lat),
        out_shape=pltpu.VMEM(prior.shape, bf16),
        in_specs=[pl.BlockSpec(memory_space=pl.ANY)] * 7,
        out_specs=pl.BlockSpec(memory_space=pltpu.VMEM),
        scratch_shapes=[
            pltpu.VMEM((3,) + prior.shape, bf16),
            pltpu.VMEM((3,) + wind.shape, f32),
            pltpu.VMEM(cell.shape, i32),
            pltpu.VMEM(value.shape, f32),
            pltpu.VMEM(prec.shape, f32),
            pltpu.VMEM(nb.shape, i32),
            pltpu.VMEM(cnt.shape, i32),
            pltpu.VMEM((5, 8, n_obs), f32),
            pltpu.VMEM((n_mem, members * rows, 4 * W), bf16),
            pltpu.VMEM((n_mem, members * rows, 4 * W), bf16),
            pltpu.VMEM((2, n_mem, members * rows, W), bf16),
            pltpu.VMEM((n_mem, members, 2, rows, W), bf16),
            dma((7,)), dma((2, 2)), dma((2, 2)), dma((4,)), dma((4,)),
            dma((3, n_mem)), dma((3, n_mem)), dma((n_mem,)), dma((n_mem,)), pltpu.SemaphoreType.REGULAR,
        ],
        compiler_params=pltpu.CompilerParams(collective_id=0, has_side_effects=True),
    )(prior, wind, cell, value, prec, nb, cnt)


def solution(mesh):
    placed = (
        P("mem", None, "lat", None),
        P(None, "lat", None),
        P("lat", "mem"),
        P("lat", "mem"),
        P("lat", "mem"),
        P("lat", "mem", None),
        P("lat", "mem"),
    )
    return jax.shard_map(
        functools.partial(on_device, mesh.shape["mem"], mesh.shape["lat"]),
        mesh=mesh,
        in_specs=placed,
        out_specs=P("mem", None, "lat", None),
        check_vma=False,
    )
```
